128 devices in a mesh: seq: 4 (over x), tp: 32 (over y, z, core).
Axes of the slice: x: 4, y: 4, z: 4, core: 2. Of those that a mesh axis runs over, the one named last changes fastest.
Arguments:
- tokens: bfloat16 [2048, 8192], P('seq', 'tp'), may hold values from -6 to 6
- cotangent: bfloat16 [2048, 8192], P('seq', 'tp'), may hold values from -6 to 6
- w_query: bfloat16 [8192, 8192], P(None, 'tp'), may hold values from -0.0625 to 0.0625
- w_key: bfloat16 [8192, 1024], P('tp'), may hold values from -0.0625 to 0.0625
- w_value: bfloat16 [8192, 1024], P('tp'), may hold values from -0.0625 to 0.0625
- mask_query: int32 [128, 128], P(None, 'tp'), may hold values 0 or 1
- mask_key: int32 [128, 16], P('tp'), may hold values 0 or 1
- mask_value: int32 [128, 16], P('tp'), may hold values 0 or 1
- documents: int32 [4, 512], P('seq'), may hold values from 0 to 7, never falling along the last dimension, each value on 1 to 256 neighbouring positions
Outputs:
- attended: bfloat16 [2048, 8192], P('seq', 'tp')
- grad_tokens: bfloat16 [2048, 8192], P('seq', 'tp')
- grad_query: bfloat16 [8192, 8192], P(None, ('tp', 'seq'))
- grad_key: bfloat16 [8192, 1024], P('tp', 'seq')
- grad_value: bfloat16 [8192, 1024], P('tp', 'seq')
The draws below stay inside these ranges and needn't reach their ends.
Inputs may be any that keep to these rules, and one draw needn't show every extreme that they name: documents never fall along a sequence; each document holds at most 256 tokens.
All inputs are finite; a program needn't handle non-finite values. No bound on the sum of `mask_query` or of `mask_key` or of `mask_value` on one device may be relied on, other than what follows from the above.
Results may differ from the reference program's by a relative error of at most 0.035.
Values may be sent and summed in bfloat16 or wider, within the bound.
A program may use at most 128 MiB of HBM per device.

```python
import math
import jax
import jax.numpy as jnp
import numpy as np
from jax import lax

D = 8192
H = 64
KVH = 8
HD = 128
BLK = 64
L = 512
SEQS = 4
TOKENS = 2048
N_TP = 32


def touch_ends(values, key, least, high):
    place = [jax.random.randint(jax.random.fold_in(key, axis), (), 0, length) for axis, length in enumerate(values.shape)]
    widest = values.shape.index(max(values.shape))
    next_to = place[:widest] + [(place[widest] + 1) % values.shape[widest]] + place[widest + 1:]
    return values.at[tuple(place)].set(least).at[tuple(next_to)].set(high)


def block_levels(rng, shape, shards, smallest, largest):
    level = 1.0
    for position, blocks in shards:
        draws = jax.random.uniform(jax.random.fold_in(jax.random.fold_in(rng, 6), position), (blocks,), jnp.float32, smallest / len(shards), largest / len(shards))
        level = level * jnp.repeat(jnp.exp(draws), shape[position] // blocks).reshape((-1,) + (1,) * (len(shape) - 1 - position))
    return level


def profile(amount, total, reach, skew):
    weights = [(1 << 20) // math.isqrt(rank ** skew) + 1 for rank in range(2, amount + 1)]
    spare, given = total - reach - (amount - 1), [1] * (amount - 1)
    while spare > 0:
        movable = [i for i in range(amount - 1) if given[i] < reach]
        pool, budget = sum([weights[i] for i in movable]), spare
        for i in movable:
            more = min(reach - given[i], max(1, budget * weights[i] // pool), spare)
            given[i] = given[i] + more
            spare = spare - more
    return np.array([reach] + given)


def uneven_parts(rng, count, total, bound, slope):
    if count == 2:
        one = jax.random.randint(rng, (), max(1, total - bound), min(bound, total - 1) + 1)
        return jnp.stack([one, total - one])
    lengths = jnp.asarray(profile(count, total, bound, slope), jnp.int32)
    pairs = (count - 1) // 2
    giver, sink = lengths[1:1 + 2 * pairs:2], lengths[2:2 + 2 * pairs:2]
    slack = jnp.minimum(giver - 1, bound - sink)
    shifted = jax.random.randint(jax.random.fold_in(rng, 1), (pairs,), 0, 1 << 20) % (slack + 1)
    lengths = lengths.at[1:1 + 2 * pairs:2].set(giver - shifted).at[2:2 + 2 * pairs:2].set(sink + shifted)
    return lengths[jax.random.permutation(jax.random.fold_in(rng, 2), count)]


def centred(key, shape, deviation, limit, cuts=(), held_as=jnp.bfloat16):
    entries = deviation * jax.random.normal(key, shape, jnp.float32)
    if cuts:
        entries = entries * block_levels(key, shape, cuts, -0.22, 0.18)
    return jnp.clip(entries, -limit, limit).astype(held_as)


def setup_inputs(seed: int = 0) -> dict:
    streams_of = jax.random.split(jax.random.key(seed), 10)
    tokens = centred(streams_of[0], (TOKENS, D), 1.0, 6.0, ((0, 4), (1, 32)))
    cotangent = centred(streams_of[1], (TOKENS, D), 1.0, 6.0, ((0, 4), (1, 32)))
    w_query = centred(streams_of[2], (D, D), D ** -0.5, 0.0625, ((1, 32),))
    w_key = centred(streams_of[3], (D, KVH * HD), D ** -0.5, 0.0625, ((0, 32),))
    w_value = centred(streams_of[4], (D, KVH * HD), D ** -0.5, 0.0625, ((0, 32),))
    mask_query = touch_ends((jax.random.randint(streams_of[5], (D // BLK, D // BLK), 0, 2) < 1).astype(jnp.int32), jax.random.fold_in(streams_of[5], 1), 0, 1)
    mask_key = touch_ends((jax.random.randint(streams_of[6], (D // BLK, KVH * HD // BLK), 0, 2) < 1).astype(jnp.int32), jax.random.fold_in(streams_of[6], 1), 0, 1)
    mask_value = touch_ends((jax.random.randint(streams_of[7], (D // BLK, KVH * HD // BLK), 0, 2) < 1).astype(jnp.int32), jax.random.fold_in(streams_of[7], 1), 0, 1)
    documents = jax.vmap(lambda own: jnp.searchsorted(jnp.cumsum(uneven_parts(own, 8, L, L // 2, 2)), jnp.arange(L), side="right"))(jax.random.split(streams_of[8], SEQS)).reshape((SEQS, L)).astype(jnp.int32)
    return {"tokens": tokens, "cotangent": cotangent, "w_query": w_query, "w_key": w_key, "w_value": w_value, "mask_query": mask_query, "mask_key": mask_key, "mask_value": mask_value, "documents": documents}


def expand(mask):
    return jnp.repeat(jnp.repeat(mask, BLK, axis=0), BLK, axis=1).astype(jnp.bfloat16)


def split_sum(left, right):
    slice_width = left.shape[1] // N_TP
    left_parts = left.reshape(left.shape[0], N_TP, slice_width).transpose(1, 0, 2)
    right_parts = right.reshape(N_TP, slice_width, right.shape[1])

    def add_part(total, pair):
        part = jnp.dot(pair[0], pair[1], preferred_element_type=jnp.float32).astype(jnp.bfloat16)
        part = lax.optimization_barrier(part).astype(jnp.float32)
        return total + part, None

    start = jnp.zeros((left.shape[0], right.shape[1]), jnp.float32)
    total, _ = lax.scan(add_part, start, (left_parts, right_parts))
    return total


def round_keep(value):
    return lax.optimization_barrier(value.astype(jnp.bfloat16)).astype(jnp.float32)


def attend(item):
    q_seq, k_seq, v_seq, g_seq, doc = item
    group_size = H // KVH
    sub_heads = min(H // N_TP, group_size)
    score_scale = HD ** -0.5
    qf = q_seq.reshape(L, H, HD).astype(jnp.float32)
    kq = jnp.repeat(k_seq.reshape(L, KVH, HD).astype(jnp.float32), group_size, axis=1)
    vq = jnp.repeat(v_seq.reshape(L, KVH, HD).astype(jnp.float32), group_size, axis=1)
    positions = jnp.arange(L)
    allowed = (doc[:, None] == doc[None, :]) & (positions[None, :] <= positions[:, None])
    scores = jnp.einsum('qhd,khd->hqk', qf, kq) * score_scale
    weights = jnp.where(allowed[None], jnp.exp(scores), 0.0)
    probs = weights / jnp.sum(weights, axis=-1, keepdims=True)
    pb = round_keep(probs)
    output = jnp.einsum('hqk,khd->qhd', pb, vq).astype(jnp.bfloat16).reshape(L, D)
    gf = g_seq.reshape(L, H, HD).astype(jnp.float32)
    dv_heads = jnp.einsum('hqk,qhd->khd', pb, gf)
    d_probs = jnp.einsum('qhd,khd->hqk', gf, vq)
    d_scores = probs * (d_probs - jnp.sum(d_probs * probs, axis=-1, keepdims=True)) * score_scale
    dsb = round_keep(d_scores)
    d_query = jnp.einsum('hqk,khd->qhd', dsb, kq).astype(jnp.bfloat16).reshape(L, D)
    dk_heads = jnp.einsum('hqk,qhd->khd', dsb, qf)
    dk_runs = dk_heads.reshape(L, H // sub_heads, sub_heads, HD).sum(axis=2).astype(jnp.bfloat16)
    dv_runs = dv_heads.reshape(L, H // sub_heads, sub_heads, HD).sum(axis=2).astype(jnp.bfloat16)
    return output, d_query, dk_runs, dv_runs


def per_sequence(left, right, mask_full):
    def add_seq(total, pair):
        term = lax.dot_general(pair[0], pair[1], (((0,), (0,)), ((), ())), preferred_element_type=jnp.float32)
        return total + round_keep(term * mask_full.astype(jnp.float32)), None

    start = jnp.zeros((left.shape[1], right.shape[1]), jnp.float32)
    total, _ = lax.scan(add_seq, start, (left.reshape(SEQS, L, left.shape[1]), right.reshape(SEQS, L, right.shape[1])))
    return total.astype(jnp.bfloat16)


def reference(tokens, cotangent, w_query, w_key, w_value, mask_query, mask_key, mask_value, documents):
    kv_width = KVH * HD
    group_size = H // KVH
    sub_heads = min(H // N_TP, group_size)
    full_q = expand(mask_query)
    full_k = expand(mask_key)
    full_v = expand(mask_value)
    mq = w_query * full_q
    mk = w_key * full_k
    mv = w_value * full_v
    query = jnp.dot(tokens, mq, preferred_element_type=jnp.float32).astype(jnp.bfloat16)
    kv = split_sum(tokens, jnp.concatenate([mk, mv], axis=1)).astype(jnp.bfloat16)
    keys = kv[:, :kv_width]
    values = kv[:, kv_width:]
    items = (query.reshape(SEQS, L, D), keys.reshape(SEQS, L, kv_width), values.reshape(SEQS, L, kv_width),
             cotangent.reshape(SEQS, L, D), documents)
    output, d_query, dk_runs, dv_runs = lax.map(attend, items)
    attended = output.reshape(TOKENS, D)
    d_query = d_query.reshape(TOKENS, D)
    runs_per_head = group_size // sub_heads
    dk_full = dk_runs.astype(jnp.float32).reshape(TOKENS, KVH, runs_per_head, HD).sum(axis=2).reshape(TOKENS, kv_width).astype(jnp.bfloat16)
    dv_full = dv_runs.astype(jnp.float32).reshape(TOKENS, KVH, runs_per_head, HD).sum(axis=2).reshape(TOKENS, kv_width).astype(jnp.bfloat16)
    grad_part = split_sum(d_query, mq.T)
    grad_part = grad_part + jnp.dot(dk_full, mk.T, preferred_element_type=jnp.float32)
    grad_part = grad_part + jnp.dot(dv_full, mv.T, preferred_element_type=jnp.float32)
    grad_tokens = grad_part.astype(jnp.bfloat16)
    grad_query = per_sequence(tokens, d_query, full_q)
    grad_key = per_sequence(tokens, dk_full, full_k)
    grad_value = per_sequence(tokens, dv_full, full_v)
    return (attended, grad_tokens, grad_query, grad_key, grad_value)
```

```python
import functools

import jax
import jax.numpy as jnp
from jax import lax
from jax.experimental import pallas as pl
from jax.experimental.pallas import tpu as pltpu
from jax.sharding import PartitionSpec as P

MESH = pl.DeviceIdType.MESH
F32 = jnp.float32
BF16 = jnp.bfloat16
HD = 128
BLK = 64
L = 512
N_SEMS = 240


def nt(a, b):
    return lax.dot_general(a, b, (((1,), (1,)), ((), ())), preferred_element_type=F32)


def tn(a, b):
    return lax.dot_general(a, b, (((0,), (0,)), ((), ())), preferred_element_type=F32)


def nn(a, b):
    return jnp.dot(a, b, preferred_element_type=F32)


def add_to(ref, idx, *terms):
    total = ref[idx].astype(F32)
    for term in terms:
        total = total + term.astype(F32)
    ref[idx] = total.astype(BF16)


def drive(gens, times=1):
    for _ in range(times):
        for g in gens:
            next(g, None)


def finish(gens):
    live = list(gens)
    while live:
        for g in list(live):
            if next(g, StopIteration) is StopIteration:
                live.remove(g)


class Links:
    def __init__(self, send_sem, recv_sem):
        self.s = lax.axis_index("seq")
        t = lax.axis_index("tp")
        self.y = lax.div(t, 8)
        self.z = lax.rem(lax.div(t, 2), 4)
        self.c = lax.rem(t, 2)
        self.send_sem, self.recv_sem = send_sem, recv_sem
        self.count = 0
        self.sent = []

    def at(self, dx=0, dy=0, dz=0, flip=False):
        x = lax.rem(self.s + (dx + 4), 4)
        y = lax.rem(self.y + (dy + 4), 4)
        z = lax.rem(self.z + (dz + 4), 4)
        c = 1 - self.c if flip else self.c
        return (x, (y * 4 + z) * 2 + c)

    def wrap(self, base, offset):
        return lax.rem(base + (offset + 8), 4)

    def send(self, src, dst, device):
        k = self.count
        self.count += 1
        copy = pltpu.make_async_remote_copy(
            src_ref=src,
            dst_ref=dst,
            send_sem=self.send_sem.at[k],
            recv_sem=self.recv_sem.at[k],
            device_id=device,
            device_id_type=MESH,
        )
        copy.start()
        self.sent.append(copy)
        return copy

    def drain(self):
        for copy in self.sent:
            copy.wait_send()


def gather_half(lk, buf, half, rows, sib):
    h, q = rows // 2, rows // 4
    base = half * h

    def slot(a, b):
        if half == 0:
            return lk.wrap(lk.y, -a), lk.wrap(lk.z, -b)
        return lk.wrap(lk.y, -b), lk.wrap(lk.z, -a)

    def ref(a, b, r0, n):
        yi, zi = slot(a, b)
        return buf.at[yi, zi, lk.c, pl.ds(base + r0, n), :]

    def near(first, step):
        along_y = first == (half == 0)
        return lk.at(dy=step) if along_y else lk.at(dz=step)

    def snd(a, b, r0, n, dev):
        return lk.send(ref(a, b, r0, n), ref(a, b, r0, n), dev)

    def across(a):
        return snd(a, 0, 0, h, near(False, 1)), snd(a, 0, 0, h, near(False, -1))

    def share(a, b):
        sib.append(snd(a, b, 0, h, lk.at(flip=True)))

    far = {}
    up = snd(0, 0, 0, h, near(True, 1))
    down = snd(0, 0, 0, h, near(True, -1))
    yield
    far[0] = across(0)
    yield
    up.wait_recv()
    up2 = snd(1, 0, 0, q, near(True, 1))
    far[1] = across(1)
    share(1, 0)
    yield
    down.wait_recv()
    down2 = snd(-1, 0, q, q, near(True, -1))
    far[-1] = across(-1)
    share(-1, 0)
    yield
    up2.wait_recv()
    down2.wait_recv()
    far[2] = across(2)
    share(2, 0)
    yield
    last = {}
    for a in (0, 1, -1, 2):
        far[a][0].wait_recv()
        one = snd(a, 1, 0, q, near(False, 1))
        share(a, 1)
        yield
        far[a][1].wait_recv()
        last[a] = one, snd(a, -1, q, q, near(False, -1))
        share(a, -1)
        yield
    for a in (0, 1, -1, 2):
        last[a][0].wait_recv()
        last[a][1].wait_recv()
        share(a, 2)
        yield


def scatter_half(lk, buf, half, rows, t1, t2, t3, t4, result):
    h, q = rows // 2, rows // 4
    base = half * h

    def group(a, r0, n):
        if half == 0:
            return buf.at[:, lk.wrap(lk.z, a), pl.ds(base + r0, n), :]
        return buf.at[lk.wrap(lk.y, a), :, pl.ds(base + r0, n), :]

    def idx(a, i, r0, n):
        if half == 0:
            return (i, lk.wrap(lk.z, a), pl.ds(base + r0, n), slice(None))
        return (lk.wrap(lk.y, a), i, pl.ds(base + r0, n), slice(None))

    def one(b, r0, n):
        if half == 0:
            return (lk.wrap(lk.y, b), lk.z, pl.ds(base + r0, n), slice(None))
        return (lk.y, lk.wrap(lk.z, b), pl.ds(base + r0, n), slice(None))

    def near(first, step):
        along_z = first == (half == 0)
        return lk.at(dz=step) if along_z else lk.at(dy=step)

    e1p = lk.send(group(2, 0, q), t1.at[half, 0], near(True, 1))
    e1m = lk.send(group(2, q, q), t1.at[half, 1], near(True, -1))
    yield
    e1p.wait_recv()
    for i in range(4):
        add_to(buf, idx(1, i, 0, q), t1[half, 0, i])
    e2p = lk.send(group(1, 0, h), t2.at[half, 0], near(True, 1))
    yield
    e1m.wait_recv()
    for i in range(4):
        add_to(buf, idx(-1, i, q, q), t1[half, 1, i])
    e2m = lk.send(group(-1, 0, h), t2.at[half, 1], near(True, -1))
    yield
    e2p.wait_recv()
    e2m.wait_recv()
    for i in range(4):
        add_to(buf, idx(0, i, 0, h), t2[half, 0, i], t2[half, 1, i])
    e3p = lk.send(buf.at[one(2, 0, q)], t3.at[half, 0], near(False, 1))
    e3m = lk.send(buf.at[one(2, q, q)], t3.at[half, 1], near(False, -1))
    yield
    e3p.wait_recv()
    add_to(buf, one(1, 0, q), t3[half, 0])
    e4p = lk.send(buf.at[one(1, 0, h)], t4.at[half, 0], near(False, 1))
    e3m.wait_recv()
    add_to(buf, one(-1, q, q), t3[half, 1])
    e4m = lk.send(buf.at[one(-1, 0, h)], t4.at[half, 1], near(False, -1))
    yield
    e4p.wait_recv()
    e4m.wait_recv()
    total = buf[one(0, 0, h)].astype(F32)
    result(base, h, total + t4[half, 0].astype(F32) + t4[half, 1].astype(F32))


class RingSum:
    def __init__(self, lk, buf, relay, final, other, way):
        self.lk, self.buf, self.way = lk, buf, way
        self.relay_buf, self.final_buf, self.other_buf = relay, final, other
        s = lk.s
        self.raw = lk.send(buf.at[lk.wrap(s, 2)], relay, lk.at(dx=way))
        self.direct = lk.send(buf.at[lk.wrap(s, -way)], other, lk.at(dx=-way))

    def relay(self):
        lk = self.lk
        self.raw.wait_recv()
        mine = lk.wrap(lk.s, self.way)
        add_to(self.buf, (mine,), self.relay_buf[...])
        self.done = lk.send(self.buf.at[mine], self.final_buf, lk.at(dx=self.way))

    def result(self):
        self.done.wait_recv()
        self.direct.wait_recv()
        total = self.buf[self.lk.s].astype(F32)
        return total + self.final_buf[...].astype(F32) + self.other_buf[...].astype(F32)


def kernel(
    tok, cot, wq_hbm, wk, wv, mask_q, mask_k, mask_v, docs,
    att, gtok, gq_out, gk_out, gv_out,
    g, mq, mqs, mkv, mw, mws, mexp, mrow, qf, qb, kvp, kvt1, kvt2, kvt3, kvt4, kvh,
    doc_col, dkf, dq, dqs, dqt, tokt, dkvp, dkvt, dkv, dx, dxt1, dxt2, dxt3, dxt4, dxkv,
    gq, gqr, gqf, gqo, gkv, gkvr, gkvf, gkvo,
    send_sem, recv_sem, local_sem,
):
    lk = Links(send_sem, recv_sem)
    y, z, c, s = lk.y, lk.z, lk.c, lk.s
    scale = HD ** (-0.5)
    zp = lax.rem(z, 2)
    z_mate = z + 1 - 2 * zp
    sibling = lk.at(flip=True)
    mate = (s, (y * 4 + z_mate) * 2 + c)
    cross = (s, (y * 4 + z_mate) * 2 + 1 - c)

    weights = pltpu.make_async_copy(wq_hbm, mq, local_sem)
    weights.start()
    barrier = pltpu.get_barrier_semaphore()
    friends = [sibling, cross, lk.at(dy=1), lk.at(dy=-1), lk.at(dz=1), lk.at(dz=-1), lk.at(dx=1), lk.at(dx=-1)]
    for friend in friends:
        pl.semaphore_signal(barrier, inc=1, device_id=friend, device_id_type=MESH)

    lane = lax.div(lax.broadcasted_iota(jnp.int32, (4, 1024), 1), BLK)
    for kind, (w, m) in enumerate(((wk, mask_k), (wv, mask_v))):
        wide = jnp.zeros((4, 1024), F32)
        for j in range(16):
            wide = jnp.where(lane == j, m[:, j : j + 1].astype(F32), wide)
        for b in range(4):
            rows = slice(b * BLK, (b + 1) * BLK)
            masked = (w[rows, :].astype(F32) * wide[b : b + 1, :]).astype(BF16)
            mw[kind, rows, :] = masked
            for head in range(8):
                mkv[head, rows, kind * HD : (kind + 1) * HD] = masked[:, head * HD : (head + 1) * HD]
    g[y, z, c] = tok[...]
    pl.semaphore_wait(barrier, len(friends))

    sib_tok = lk.send(tok, g.at[y, z, c], sibling)
    sib_w = lk.send(mw.at[1 - c], mws, sibling)
    shared = []
    ga = gather_half(lk, g, 0, L, shared)
    gb = gather_half(lk, g, 1, L, shared)
    drive((ga, gb), 2)

    lane = lax.div(lax.broadcasted_iota(jnp.int32, (128, 256), 1), BLK)
    col = lax.broadcasted_iota(jnp.int32, (128, 4), 1)
    wide = jnp.zeros((128, 256), F32)
    for j in range(4):
        wide = jnp.where(lane == j, mask_q[:, j : j + 1].astype(F32), wide)
    mexp[...] = wide
    own_col = jnp.sum(jnp.where(col == s, mask_q[...].astype(F32), 0.0), axis=1, keepdims=True)
    mrow[...] = jnp.broadcast_to(own_col, (128, 128))
    weights.wait()

    def mask_chunk(t, carry):
        yi, zi, ci = lax.div(t, 8), lax.rem(lax.div(t, 2), 4), lax.rem(t, 2)
        for b in range(4):
            rows = slice(b * BLK, (b + 1) * BLK)
            line = mexp[pl.ds(4 * t + b, 1), :]
            mq[yi, zi, ci, rows, :] = (mq[yi, zi, ci, rows, :].astype(F32) * line).astype(BF16)
        return carry

    lax.fori_loop(0, 32, mask_chunk, 0)
    sib_mq = lk.send(mq.at[:, :, 1 - c], mqs, sibling)

    sib_tok.wait_recv()
    sib_w.wait_recv()

    def kv_pair(i, carry):
        cols = pl.ds(pl.multiple_of(i * 256, 256), 256)
        part = nn(tok[...], mw[c, :, cols]) + nn(g[y, z, 1 - c], mws[:, cols])
        part = part.astype(BF16)
        for hh in range(2):
            for th in range(2):
                kvp[i, 2 * hh + th] = part[th * 256 : (th + 1) * 256, hh * HD : (hh + 1) * HD]
        return carry

    lax.fori_loop(0, 4, kv_pair, 0)

    def store_kv(base, n, value):
        kvh[c, zp, base : base + n, :] = value.astype(BF16)

    ka = scatter_half(lk, kvp, 0, 256, kvt1, kvt2, kvt3, kvt4, store_kv)
    kb = scatter_half(lk, kvp, 1, 256, kvt1, kvt2, kvt3, kvt4, store_kv)
    drive((ka, kb))
    drive((ga, gb), 3)
    drive((ka, kb), 2)

    qf[...] = jnp.zeros_like(qf)

    def project(yi, zi, ci):
        qf[...] += nn(g[yi, zi, ci], mq[yi, zi, ci])

    project(y, z, c)
    project(y, z, 1 - c)
    drive((ga, gb), 2)
    drive((ka, kb))
    drive((ga, gb), 2)
    finish((ka, kb))
    hand = [lk.send(kvh.at[c, zp], kvh.at[c, zp], dev) for dev in (sibling, mate, cross)]
    tokt[...] = tok[...].astype(F32).T.astype(BF16)
    finish((ga, gb))

    def project_own(i, carry):
        yi, zi = lax.div(i, 4), lax.rem(i, 4)
        project(lk_wrap(y, yi), lk_wrap(z, zi), c)
        return carry

    def lk_wrap(base, offset):
        return lax.rem(base + offset, 4)

    lax.fori_loop(1, 16, project_own, 0)
    for copy in shared:
        copy.wait_recv()

    def project_sib(i, carry):
        yi, zi = lax.div(i, 4), lax.rem(i, 4)
        project(lk_wrap(y, yi), lk_wrap(z, zi), 1 - c)
        return carry

    lax.fori_loop(1, 16, project_sib, 0)
    qb[...] = qf[...].astype(BF16)
    for copy in hand:
        copy.wait_recv()

    doc_row = docs[...]
    doc_col[...] = jnp.broadcast_to(doc_row.astype(F32), (128, L)).T
    for h in range(2):
        hs = slice(h * HD, (h + 1) * HD)
        for rb in (1, 0):
            rows, nk = slice(rb * 256, rb * 256 + 256), rb * 256 + 256
            kk = kvh[0].reshape(L, HD)[:nk]
            vv = kvh[1].reshape(L, HD)[:nk]
            qh, gh = qb[rows, hs], cot[rows, hs]
            ri = lax.broadcasted_iota(jnp.int32, (256, nk), 0) + rb * 256
            ci = lax.broadcasted_iota(jnp.int32, (256, nk), 1)
            same = doc_col[rows, 0:1] == doc_row[:, :nk].astype(F32)
            allowed = jnp.logical_and(same, ci <= ri)
            w = jnp.where(allowed, jnp.exp(nt(qh, kk) * scale), 0.0)
            probs = w * (1.0 / jnp.sum(w, axis=1, keepdims=True))
            pb = probs.astype(BF16)
            att[rows, hs] = nn(pb, vv).astype(BF16)
            da = nt(gh, vv)
            ds = probs * (da - jnp.sum(da * probs, axis=1, keepdims=True)) * scale
            ds = ds.astype(BF16)
            dq[rows, hs] = nn(ds, kk).astype(BF16)
            dk_part, dv_part = tn(ds, qh), tn(pb, gh)
            if h == 0 and rb == 1:
                dkf[:nk, :HD] = dk_part
                dkf[:nk, HD:] = dv_part
            else:
                dkf[:nk, :HD] += dk_part
                dkf[:nk, HD:] += dv_part
    dkvp[...] = dkf[...].astype(BF16).reshape(4, 128, 256)

    sib_dq = lk.send(dq, dqs, sibling)
    quarter = 2 * zp + c
    swaps = []
    for i, (dev, qi) in enumerate(
        ((sibling, 2 * zp + 1 - c), (mate, 2 * (1 - zp) + c), (cross, 2 * (1 - zp) + 1 - c))
    ):
        swaps.append(lk.send(dkvp.at[qi], dkvt.at[i], dev))
    dqt[...] = dq[...].astype(F32).T.astype(BF16)

    rings = []

    def grad_query_group(j):
        for i in range(4):
            t = 4 * j + i
            part = nn(dqt[...], g[t // 8, (t // 2) % 4, t % 2]).astype(BF16)
            gq[j, :, :, i * 256 : (i + 1) * 256] = part.reshape(4, BLK, 256)
        rings.append(RingSum(lk, gq.at[j], gqr.at[j], gqf.at[j], gqo.at[j], 1 - 2 * (j % 2)))

    grad_query_group(0)
    grad_query_group(1)
    for copy in swaps:
        copy.wait_recv()
    total = dkvp[quarter].astype(F32)
    for i in range(3):
        total = total + dkvt[i].astype(F32)
    dkv[y, z, c] = total.astype(BF16)
    shared2 = [lk.send(dkv.at[y, z, c], dkv.at[y, z, c], sibling)]
    da_ = gather_half(lk, dkv, 0, 128, shared2)
    db_ = gather_half(lk, dkv, 1, 128, shared2)
    drive((da_, db_), 2)
    grad_query_group(2)
    grad_query_group(3)
    grad_query_group(4)
    drive((da_, db_), 2)
    grad_query_group(5)
    grad_query_group(6)
    grad_query_group(7)
    drive((da_, db_), 1)

    sib_mq.wait_recv()
    sib_dq.wait_recv()

    def dx_slot(yi, zi):
        part = nt(dq[...], mq[yi, zi, c]) + nt(dqs[...], mqs[yi, zi])
        dx[yi, zi] = part.astype(BF16)

    def dx_far_z(i, carry):
        dx_slot(i, lk_wrap(z, 2))
        return carry

    def dx_far_y(i, carry):
        dx_slot(lk_wrap(y, 2), lk_wrap(z, 2 + i))
        return carry

    def dx_near(i, carry):
        dx_slot(lk_wrap(y, 3 + lax.div(i, 3)), lk_wrap(z, 3 + lax.rem(i, 3)))
        return carry

    def store_dx(base, n, value):
        rows = slice(base, base + n)
        gtok[rows, :] = (value + dxkv[rows, :]).astype(BF16)

    xa = scatter_half(lk, dx, 0, L, dxt1, dxt2, dxt3, dxt4, store_dx)
    xb = scatter_half(lk, dx, 1, L, dxt1, dxt2, dxt3, dxt4, store_dx)
    lax.fori_loop(0, 4, dx_far_z, 0)
    drive((xa,))
    lax.fori_loop(1, 4, dx_far_y, 0)
    drive((xb,))
    lax.fori_loop(0, 9, dx_near, 0)
    drive((da_, db_), 4)
    drive((xa, xb))
    drive((da_, db_), 4)
    drive((xa, xb))
    rings[0].relay()
    rings[1].relay()
    finish((da_, db_))
    for copy in shared2:
        copy.wait_recv()

    for p in range(4):
        for hh in range(2):
            zi = 2 * hh
            pair = jnp.concatenate(
                [dkv[p, zi, 0], dkv[p, zi, 1], dkv[p, zi + 1, 0], dkv[p, zi + 1, 1]], axis=0
            )
            part = nn(tokt[...], pair).astype(BF16)
            gkv[0, p, :, hh * HD : (hh + 1) * HD] = part[:, :HD]
            gkv[1, p, :, hh * HD : (hh + 1) * HD] = part[:, HD:]
            more = nt(pair, mkv[2 * p + hh])
            if p == 0 and hh == 0:
                dxkv[...] = more
            else:
                dxkv[...] += more
    kv_rings = [
        RingSum(lk, gkv.at[i], gkvr.at[i], gkvf.at[i], gkvo.at[i], 1 - 2 * i) for i in range(2)
    ]
    for ring in rings[2:4]:
        ring.relay()
    drive((xa, xb))
    for ring in rings[4:6]:
        ring.relay()
    drive((xa, xb))
    for ring in rings[6:8]:
        ring.relay()
    finish((xa, xb))
    for ring in kv_rings:
        ring.relay()
    for j, ring in enumerate(rings):
        turned = ring.result().T
        for b in range(16):
            line = mrow[16 * j + b : 16 * j + b + 1, :BLK]
            rows = slice(j * 1024 + b * BLK, j * 1024 + (b + 1) * BLK)
            gq_out[rows, :] = (turned[b * BLK : (b + 1) * BLK, :] * line).astype(BF16)
    lane = lax.div(lax.broadcasted_iota(jnp.int32, (4, 256), 1), BLK)
    col = lax.broadcasted_iota(jnp.int32, (4, 16), 1)
    for ring, m, out in ((kv_rings[0], mask_k, gk_out), (kv_rings[1], mask_v, gv_out)):
        wide = jnp.zeros((4, 256), F32)
        for j in range(4):
            pick = jnp.sum(jnp.where(col == 4 * s + j, m[...].astype(F32), 0.0), axis=1, keepdims=True)
            wide = jnp.where(lane == j, pick, wide)
        total = ring.result()
        for b in range(4):
            rows = slice(b * BLK, (b + 1) * BLK)
            out[rows, :] = (total[rows, :] * wide[b : b + 1, :]).astype(BF16)
    lk.drain()


def on_device(tokens, cotangent, w_query, w_key, w_value, mask_query, mask_key, mask_value, documents):
    vmem = pl.BlockSpec(memory_space=pltpu.VMEM)
    any_space = pl.BlockSpec(memory_space=pl.ANY)
    dma = pltpu.SemaphoreType.DMA
    scratch = [
        ((4, 4, 2, 512, 256), BF16),
        ((4, 4, 2, 256, 256), BF16),
        ((4, 4, 256, 256), BF16),
        ((8, 256, 256), BF16),
        ((2, 256, 1024), BF16),
        ((256, 1024), BF16),
        ((128, 256), F32),
        ((128, 128), F32),
        ((512, 256), F32),
        ((512, 256), BF16),
        ((4, 4, 256, 128), BF16),
        ((2, 2, 4, 64, 128), BF16),
        ((2, 2, 4, 128, 128), BF16),
        ((2, 2, 64, 128), BF16),
        ((2, 2, 128, 128), BF16),
        ((2, 2, 256, 128), BF16),
        ((512, 128), F32),
        ((512, 256), F32),
        ((512, 256), BF16),
        ((512, 256), BF16),
        ((256, 512), BF16),
        ((256, 512), BF16),
        ((4, 128, 256), BF16),
        ((3, 128, 256), BF16),
        ((4, 4, 2, 128, 256), BF16),
        ((4, 4, 512, 256), BF16),
        ((2, 2, 4, 128, 256), BF16),
        ((2, 2, 4, 256, 256), BF16),
        ((2, 2, 128, 256), BF16),
        ((2, 2, 256, 256), BF16),
        ((512, 256), F32),
        ((8, 4, 64, 1024), BF16),
        ((8, 64, 1024), BF16),
        ((8, 64, 1024), BF16),
        ((8, 64, 1024), BF16),
        ((2, 4, 256, 256), BF16),
        ((2, 256, 256), BF16),
        ((2, 256, 256), BF16),
        ((2, 256, 256), BF16),
    ]
    return pl.pallas_call(
        kernel,
        name="step",
        out_shape=(
            jax.ShapeDtypeStruct((512, 256), BF16),
            jax.ShapeDtypeStruct((512, 256), BF16),
            jax.ShapeDtypeStruct((8192, 64), BF16),
            jax.ShapeDtypeStruct((256, 256), BF16),
            jax.ShapeDtypeStruct((256, 256), BF16),
        ),
        in_specs=[vmem, vmem, any_space] + [vmem] * 6,
        out_specs=(vmem,) * 5,
        scratch_shapes=[pltpu.VMEM(shape, dtype) for shape, dtype in scratch]
        + [dma((N_SEMS,)), dma((N_SEMS,)), dma],
        compiler_params=pltpu.CompilerParams(
            collective_id=0, has_side_effects=True, vmem_limit_bytes=67043328
        ),
    )(
        tokens, cotangent, w_query.reshape(4, 4, 2, 256, 256), w_key, w_value,
        mask_query, mask_key, mask_value, documents,
    )


def solution(mesh):
    in_specs = (
        P("seq", "tp"),
        P("seq", "tp"),
        P(None, "tp"),
        P("tp", None),
        P("tp", None),
        P(None, "tp"),
        P("tp", None),
        P("tp", None),
        P("seq", None),
    )
    out_specs = (
        P("seq", "tp"),
        P("seq", "tp"),
        P(None, ("tp", "seq")),
        P("tp", "seq"),
        P("tp", "seq"),
    )
    return jax.shard_map(
        on_device, mesh=mesh, in_specs=in_specs, out_specs=out_specs, check_vma=False
    )
```

```python
import functools

import jax
import jax.numpy as jnp
from jax import lax
from jax.experimental import pallas as pl
from jax.experimental.pallas import tpu as pltpu
from jax.sharding import PartitionSpec as P

MESH = pl.DeviceIdType.MESH
F32 = jnp.float32
BF16 = jnp.bfloat16
HD = 128
BLK = 64
L = 512
N_SEMS = 240


def nt(a, b):
    return lax.dot_general(a, b, (((1,), (1,)), ((), ())), preferred_element_type=F32)


def tn(a, b):
    return lax.dot_general(a, b, (((0,), (0,)), ((), ())), preferred_element_type=F32)


def nn(a, b):
    return jnp.dot(a, b, preferred_element_type=F32)


def add_to(ref, idx, *terms):
    total = ref[idx].astype(F32)
    for term in terms:
        total = total + term.astype(F32)
    ref[idx] = total.astype(BF16)


def drive(gens, times=1):
    for _ in range(times):
        for g in gens:
            next(g, None)


def finish(gens):
    live = list(gens)
    while live:
        for g in list(live):
            if next(g, StopIteration) is StopIteration:
                live.remove(g)


class Links:
    def __init__(self, send_sem, recv_sem):
        self.s = lax.axis_index("seq")
        t = lax.axis_index("tp")
        self.y = lax.div(t, 8)
        self.z = lax.rem(lax.div(t, 2), 4)
        self.c = lax.rem(t, 2)
        self.send_sem, self.recv_sem = send_sem, recv_sem
        self.count = 0
        self.sent = []

    def at(self, dx=0, dy=0, dz=0, flip=False):
        x = lax.rem(self.s + (dx + 4), 4)
        y = lax.rem(self.y + (dy + 4), 4)
        z = lax.rem(self.z + (dz + 4), 4)
        c = 1 - self.c if flip else self.c
        return (x, (y * 4 + z) * 2 + c)

    def wrap(self, base, offset):
        return lax.rem(base + (offset + 8), 4)

    def send(self, src, dst, device):
        k = self.count
        self.count += 1
        copy = pltpu.make_async_remote_copy(
            src_ref=src,
            dst_ref=dst,
            send_sem=self.send_sem.at[k],
            recv_sem=self.recv_sem.at[k],
            device_id=device,
            device_id_type=MESH,
        )
        copy.start()
        self.sent.append(copy)
        return copy

    def drain(self):
        for copy in self.sent:
            copy.wait_send()


def gather_half(lk, buf, half, rows, sib):
    h, q = rows // 2, rows // 4
    base = half * h

    def slot(a, b):
        if half == 0:
            return lk.wrap(lk.y, -a), lk.wrap(lk.z, -b)
        return lk.wrap(lk.y, -b), lk.wrap(lk.z, -a)

    def ref(a, b, r0, n):
        yi, zi = slot(a, b)
        return buf.at[yi, zi, lk.c, pl.ds(base + r0, n), :]

    def near(first, step):
        along_y = first == (half == 0)
        return lk.at(dy=step) if along_y else lk.at(dz=step)

    def snd(a, b, r0, n, dev):
        return lk.send(ref(a, b, r0, n), ref(a, b, r0, n), dev)

    def across(a):
        return snd(a, 0, 0, h, near(False, 1)), snd(a, 0, 0, h, near(False, -1))

    def share(a, b):
        sib.append(snd(a, b, 0, h, lk.at(flip=True)))

    far = {}
    up = snd(0, 0, 0, h, near(True, 1))
    down = snd(0, 0, 0, h, near(True, -1))
    yield
    far[0] = across(0)
    yield
    up.wait_recv()
    up2 = snd(1, 0, 0, q, near(True, 1))
    far[1] = across(1)
    share(1, 0)
    yield
    down.wait_recv()
    down2 = snd(-1, 0, q, q, near(True, -1))
    far[-1] = across(-1)
    share(-1, 0)
    yield
    up2.wait_recv()
    down2.wait_recv()
    far[2] = across(2)
    share(2, 0)
    yield
    last = {}
    for a in (0, 1, -1, 2):
        far[a][0].wait_recv()
        one = snd(a, 1, 0, q, near(False, 1))
        share(a, 1)
        yield
        far[a][1].wait_recv()
        last[a] = one, snd(a, -1, q, q, near(False, -1))
        share(a, -1)
        yield
    for a in (0, 1, -1, 2):
        last[a][0].wait_recv()
        last[a][1].wait_recv()
        share(a, 2)
        yield


def scatter_half(lk, buf, half, rows, t1, t2, t3, t4, result):
    h, q = rows // 2, rows // 4
    base = half * h

    def group(a, r0, n):
        if half == 0:
            return buf.at[:, lk.wrap(lk.z, a), pl.ds(base + r0, n), :]
        return buf.at[lk.wrap(lk.y, a), :, pl.ds(base + r0, n), :]

    def idx(a, i, r0, n):
        if half == 0:
            return (i, lk.wrap(lk.z, a), pl.ds(base + r0, n), slice(None))
        return (lk.wrap(lk.y, a), i, pl.ds(base + r0, n), slice(None))

    def one(b, r0, n):
        if half == 0:
            return (lk.wrap(lk.y, b), lk.z, pl.ds(base + r0, n), slice(None))
        return (lk.y, lk.wrap(lk.z, b), pl.ds(base + r0, n), slice(None))

    def near(first, step):
        along_z = first == (half == 0)
        return lk.at(dz=step) if along_z else lk.at(dy=step)

    e1p = lk.send(group(2, 0, q), t1.at[half, 0], near(True, 1))
    e1m = lk.send(group(2, q, q), t1.at[half, 1], near(True, -1))
    yield
    e1p.wait_recv()
    for i in range(4):
        add_to(buf, idx(1, i, 0, q), t1[half, 0, i])
    e2p = lk.send(group(1, 0, h), t2.at[half, 0], near(True, 1))
    yield
    e1m.wait_recv()
    for i in range(4):
        add_to(buf, idx(-1, i, q, q), t1[half, 1, i])
    e2m = lk.send(group(-1, 0, h), t2.at[half, 1], near(True, -1))
    yield
    e2p.wait_recv()
    e2m.wait_recv()
    for i in range(4):
        add_to(buf, idx(0, i, 0, h), t2[half, 0, i], t2[half, 1, i])
    e3p = lk.send(buf.at[one(2, 0, q)], t3.at[half, 0], near(False, 1))
    e3m = lk.send(buf.at[one(2, q, q)], t3.at[half, 1], near(False, -1))
    yield
    e3p.wait_recv()
    add_to(buf, one(1, 0, q), t3[half, 0])
    e4p = lk.send(buf.at[one(1, 0, h)], t4.at[half, 0], near(False, 1))
    e3m.wait_recv()
    add_to(buf, one(-1, q, q), t3[half, 1])
    e4m = lk.send(buf.at[one(-1, 0, h)], t4.at[half, 1], near(False, -1))
    yield
    e4p.wait_recv()
    e4m.wait_recv()
    total = buf[one(0, 0, h)].astype(F32)
    result(base, h, total + t4[half, 0].astype(F32) + t4[half, 1].astype(F32))


class RingSum:
    def __init__(self, lk, buf, relay, final, other, way):
        self.lk, self.buf, self.way = lk, buf, way
        self.relay_buf, self.final_buf, self.other_buf = relay, final, other
        s = lk.s
        self.raw = lk.send(buf.at[lk.wrap(s, 2)], relay, lk.at(dx=way))
        self.direct = lk.send(buf.at[lk.wrap(s, -way)], other, lk.at(dx=-way))

    def relay(self):
        lk = self.lk
        self.raw.wait_recv()
        mine = lk.wrap(lk.s, self.way)
        add_to(self.buf, (mine,), self.relay_buf[...])
        self.done = lk.send(self.buf.at[mine], self.final_buf, lk.at(dx=self.way))

    def result(self):
        self.done.wait_recv()
        self.direct.wait_recv()
        total = self.buf[self.lk.s].astype(F32)
        return total + self.final_buf[...].astype(F32) + self.other_buf[...].astype(F32)


def kernel(
    tok, cot, wq_hbm, wk, wv, mask_q, mask_k, mask_v, docs,
    att, gtok, gq_out, gk_out, gv_out,
    g, mq, mqs, mkv, mw, mws, mexp, mrow, qf, qb, kvp, kvt1, kvt2, kvt3, kvt4, kvh,
    doc_col, dkf, dq, dqs, dqt, tokt, dkvp, dkvt, dkv, dx, dxt1, dxt2, dxt3, dxt4, dxkv,
    gq, gqr, gqf, gqo, gkv, gkvr, gkvf, gkvo,
    send_sem, recv_sem, local_sem,
):
    lk = Links(send_sem, recv_sem)
    y, z, c, s = lk.y, lk.z, lk.c, lk.s
    scale = HD ** (-0.5)
    zp = lax.rem(z, 2)
    z_mate = z + 1 - 2 * zp
    sibling = lk.at(flip=True)
    mate = (s, (y * 4 + z_mate) * 2 + c)
    cross = (s, (y * 4 + z_mate) * 2 + 1 - c)

    weights = pltpu.make_async_copy(wq_hbm, mq, local_sem)
    weights.start()
    barrier = pltpu.get_barrier_semaphore()
    friends = [sibling, cross, lk.at(dy=1), lk.at(dy=-1), lk.at(dz=1), lk.at(dz=-1), lk.at(dx=1), lk.at(dx=-1)]
    for friend in friends:
        pl.semaphore_signal(barrier, inc=1, device_id=friend, device_id_type=MESH)

    lane = lax.div(lax.broadcasted_iota(jnp.int32, (4, 1024), 1), BLK)
    for kind, (w, m) in enumerate(((wk, mask_k), (wv, mask_v))):
        wide = jnp.zeros((4, 1024), F32)
        for j in range(16):
            wide = jnp.where(lane == j, m[:, j : j + 1].astype(F32), wide)
        for b in range(4):
            rows = slice(b * BLK, (b + 1) * BLK)
            masked = (w[rows, :].astype(F32) * wide[b : b + 1, :]).astype(BF16)
            mw[kind, rows, :] = masked
            for head in range(8):
                mkv[head, rows, kind * HD : (kind + 1) * HD] = masked[:, head * HD : (head + 1) * HD]
    g[y, z, c] = tok[...]
    pl.semaphore_wait(barrier, len(friends))

    sib_tok = lk.send(tok, g.at[y, z, c], sibling)
    sib_w = lk.send(mw.at[1 - c], mws, sibling)
    shared = []
    ga = gather_half(lk, g, 0, L, shared)
    gb = gather_half(lk, g, 1, L, shared)
    drive((ga, gb), 2)

    lane = lax.div(lax.broadcasted_iota(jnp.int32, (128, 256), 1), BLK)
    row = lax.broadcasted_iota(jnp.int32, (128, 128), 0)
    cols = jnp.zeros((128, 128), F32)
    own = jnp.zeros((8, 128), F32)
    for j in range(4):
        line = mask_q[j : j + 1, :].astype(F32)
        cols = jnp.where(row == j, line, cols)
        own = jnp.where(s == j, line, own)
    cols = cols.T
    wide = jnp.zeros((128, 256), F32)
    for j in range(4):
        wide = jnp.where(lane == j, cols[:, j : j + 1], wide)
    mexp[...] = wide
    own = own.astype(BF16)
    ahead = lax.broadcasted_iota(jnp.int32, (128, 1024), 0) - lax.div(
        lax.broadcasted_iota(jnp.int32, (128, 1024), 1), BLK
    )
    for j in range(8):
        mrow[:, j * 1024 : (j + 1) * 1024] = nn(own, jnp.where(ahead == 16 * j, 1.0, 0.0).astype(BF16))
    weights.wait()

    def mask_chunk(t, carry):
        yi, zi, ci = lax.div(t, 8), lax.rem(lax.div(t, 2), 4), lax.rem(t, 2)
        for b in range(4):
            rows = slice(b * BLK, (b + 1) * BLK)
            line = mexp[pl.ds(4 * t + b, 1), :]
            mq[yi, zi, ci, rows, :] = (mq[yi, zi, ci, rows, :].astype(F32) * line).astype(BF16)
        return carry

    lax.fori_loop(0, 32, mask_chunk, 0)
    sib_mq = lk.send(mq.at[:, :, 1 - c], mqs, sibling)

    sib_tok.wait_recv()
    sib_w.wait_recv()

    def kv_pair(i, carry):
        cols = pl.ds(pl.multiple_of(i * 256, 256), 256)
        part = nn(tok[...], mw[c, :, cols]) + nn(g[y, z, 1 - c], mws[:, cols])
        part = part.astype(BF16)
        for hh in range(2):
            for th in range(2):
                kvp[i, 2 * hh + th] = part[th * 256 : (th + 1) * 256, hh * HD : (hh + 1) * HD]
        return carry

    lax.fori_loop(0, 4, kv_pair, 0)

    def store_kv(base, n, value):
        kvh[c, zp, base : base + n, :] = value.astype(BF16)

    ka = scatter_half(lk, kvp, 0, 256, kvt1, kvt2, kvt3, kvt4, store_kv)
    kb = scatter_half(lk, kvp, 1, 256, kvt1, kvt2, kvt3, kvt4, store_kv)
    drive((ka, kb))
    drive((ga, gb), 3)
    drive((ka, kb), 2)

    qf[...] = jnp.zeros_like(qf)

    def project(yi, zi, ci):
        qf[...] += nn(g[yi, zi, ci], mq[yi, zi, ci])

    project(y, z, c)
    project(y, z, 1 - c)
    drive((ga, gb), 2)
    drive((ka, kb))
    drive((ga, gb), 2)
    finish((ka, kb))
    hand = [lk.send(kvh.at[c, zp], kvh.at[c, zp], dev) for dev in (sibling, mate, cross)]
    tokt[...] = tok[...].astype(F32).T.astype(BF16)
    finish((ga, gb))

    def project_own(i, carry):
        yi, zi = lax.div(i, 4), lax.rem(i, 4)
        project(lk_wrap(y, yi), lk_wrap(z, zi), c)
        return carry

    def lk_wrap(base, offset):
        return lax.rem(base + offset, 4)

    lax.fori_loop(1, 16, project_own, 0)
    for copy in shared:
        copy.wait_recv()

    def project_sib(i, carry):
        yi, zi = lax.div(i, 4), lax.rem(i, 4)
        project(lk_wrap(y, yi), lk_wrap(z, zi), 1 - c)
        return carry

    lax.fori_loop(1, 16, project_sib, 0)
    qb[...] = qf[...].astype(BF16)
    for copy in hand:
        copy.wait_recv()

    doc_row = docs[...]
    doc_col[...] = jnp.broadcast_to(doc_row.astype(F32), (128, L)).T
    for h in range(2):
        hs = slice(h * HD, (h + 1) * HD)
        for rb in (1, 0):
            rows, nk = slice(rb * 256, rb * 256 + 256), rb * 256 + 256
            kk = kvh[0].reshape(L, HD)[:nk]
            vv = kvh[1].reshape(L, HD)[:nk]
            qh, gh = qb[rows, hs], cot[rows, hs]
            ri = lax.broadcasted_iota(jnp.int32, (256, nk), 0) + rb * 256
            ci = lax.broadcasted_iota(jnp.int32, (256, nk), 1)
            same = doc_col[rows, 0:1] == doc_row[:, :nk].astype(F32)
            allowed = jnp.logical_and(same, ci <= ri)
            w = jnp.where(allowed, jnp.exp(nt(qh, kk) * scale), 0.0)
            probs = w * (1.0 / jnp.sum(w, axis=1, keepdims=True))
            pb = probs.astype(BF16)
            att[rows, hs] = nn(pb, vv).astype(BF16)
            da = nt(gh, vv)
            ds = probs * (da - jnp.sum(da * probs, axis=1, keepdims=True)) * scale
            ds = ds.astype(BF16)
            dq[rows, hs] = nn(ds, kk).astype(BF16)
            dk_part, dv_part = tn(ds, qh), tn(pb, gh)
            if h == 0 and rb == 1:
                dkf[:nk, :HD] = dk_part
                dkf[:nk, HD:] = dv_part
            else:
                dkf[:nk, :HD] += dk_part
                dkf[:nk, HD:] += dv_part
    dkvp[...] = dkf[...].astype(BF16).reshape(4, 128, 256)

    sib_dq = lk.send(dq, dqs, sibling)
    quarter = 2 * zp + c
    swaps = []
    for i, (dev, qi) in enumerate(
        ((sibling, 2 * zp + 1 - c), (mate, 2 * (1 - zp) + c), (cross, 2 * (1 - zp) + 1 - c))
    ):
        swaps.append(lk.send(dkvp.at[qi], dkvt.at[i], dev))
    dqt[...] = dq[...].astype(F32).T.astype(BF16)

    rings = []

    def grad_query_group(j):
        for i in range(4):
            t = 4 * j + i
            part = nn(dqt[...], g[t // 8, (t // 2) % 4, t % 2]).astype(BF16)
            gq[j, :, :, i * 256 : (i + 1) * 256] = part.reshape(4, BLK, 256)
        rings.append(RingSum(lk, gq.at[j], gqr.at[j], gqf.at[j], gqo.at[j], 1 - 2 * (j % 2)))

    grad_query_group(0)
    grad_query_group(1)
    for copy in swaps:
        copy.wait_recv()
    total = dkvp[quarter].astype(F32)
    for i in range(3):
        total = total + dkvt[i].astype(F32)
    dkv[y, z, c] = total.astype(BF16)
    shared2 = [lk.send(dkv.at[y, z, c], dkv.at[y, z, c], sibling)]
    da_ = gather_half(lk, dkv, 0, 128, shared2)
    db_ = gather_half(lk, dkv, 1, 128, shared2)
    drive((da_, db_), 2)
    grad_query_group(2)
    grad_query_group(3)
    grad_query_group(4)
    drive((da_, db_), 2)
    grad_query_group(5)
    grad_query_group(6)
    grad_query_group(7)
    drive((da_, db_), 1)

    sib_mq.wait_recv()
    sib_dq.wait_recv()

    def dx_slot(yi, zi):
        part = nt(dq[...], mq[yi, zi, c]) + nt(dqs[...], mqs[yi, zi])
        dx[yi, zi] = part.astype(BF16)

    def dx_far_z(i, carry):
        dx_slot(i, lk_wrap(z, 2))
        return carry

    def dx_far_y(i, carry):
        dx_slot(lk_wrap(y, 2), lk_wrap(z, 2 + i))
        return carry

    def dx_near(i, carry):
        dx_slot(lk_wrap(y, 3 + lax.div(i, 3)), lk_wrap(z, 3 + lax.rem(i, 3)))
        return carry

    def store_dx(base, n, value):
        rows = slice(base, base + n)
        gtok[rows, :] = (value + dxkv[rows, :]).astype(BF16)

    xa = scatter_half(lk, dx, 0, L, dxt1, dxt2, dxt3, dxt4, store_dx)
    xb = scatter_half(lk, dx, 1, L, dxt1, dxt2, dxt3, dxt4, store_dx)
    lax.fori_loop(0, 4, dx_far_z, 0)
    drive((xa,))
    lax.fori_loop(1, 4, dx_far_y, 0)
    drive((xb,))
    lax.fori_loop(0, 9, dx_near, 0)
    drive((da_, db_), 4)
    drive((xa, xb))
    drive((da_, db_), 4)
    drive((xa, xb))
    rings[0].relay()
    rings[1].relay()
    finish((da_, db_))
    for copy in shared2:
        copy.wait_recv()

    for p in range(4):
        for hh in range(2):
            zi = 2 * hh
            pair = jnp.concatenate(
                [dkv[p, zi, 0], dkv[p, zi, 1], dkv[p, zi + 1, 0], dkv[p, zi + 1, 1]], axis=0
            )
            part = nn(tokt[...], pair).astype(BF16)
            gkv[0, p, :, hh * HD : (hh + 1) * HD] = part[:, :HD]
            gkv[1, p, :, hh * HD : (hh + 1) * HD] = part[:, HD:]
            more = nt(pair, mkv[2 * p + hh])
            if p == 0 and hh == 0:
                dxkv[...] = more
            else:
                dxkv[...] += more
    kv_rings = [
        RingSum(lk, gkv.at[i], gkvr.at[i], gkvf.at[i], gkvo.at[i], 1 - 2 * i) for i in range(2)
    ]
    for ring in rings[2:4]:
        ring.relay()
    drive((xa, xb))
    for ring in rings[4:6]:
        ring.relay()
    drive((xa, xb))
    for ring in rings[6:8]:
        ring.relay()
    finish((xa, xb))
    for ring in kv_rings:
        ring.relay()
    for j, ring in enumerate(rings):
        cols = slice(j * 1024, (j + 1) * 1024)
        gq_out[:, cols] = (ring.result() * mrow[0:1, cols]).astype(BF16)
    lane = lax.div(lax.broadcasted_iota(jnp.int32, (4, 256), 1), BLK)
    col = lax.broadcasted_iota(jnp.int32, (4, 16), 1)
    for ring, m, out in ((kv_rings[0], mask_k, gk_out), (kv_rings[1], mask_v, gv_out)):
        wide = jnp.zeros((4, 256), F32)
        for j in range(4):
            pick = jnp.sum(jnp.where(col == 4 * s + j, m[...].astype(F32), 0.0), axis=1, keepdims=True)
            wide = jnp.where(lane == j, pick, wide)
        total = ring.result()
        for b in range(4):
            rows = slice(b * BLK, (b + 1) * BLK)
            out[rows, :] = (total[rows, :] * wide[b : b + 1, :]).astype(BF16)
    lk.drain()


def on_device(tokens, cotangent, w_query, w_key, w_value, mask_query, mask_key, mask_value, documents):
    vmem = pl.BlockSpec(memory_space=pltpu.VMEM)
    any_space = pl.BlockSpec(memory_space=pl.ANY)
    dma = pltpu.SemaphoreType.DMA
    scratch = [
        ((4, 4, 2, 512, 256), BF16),
        ((4, 4, 2, 256, 256), BF16),
        ((4, 4, 256, 256), BF16),
        ((8, 256, 256), BF16),
        ((2, 256, 1024), BF16),
        ((256, 1024), BF16),
        ((128, 256), F32),
        ((8, 8192), F32),
        ((512, 256), F32),
        ((512, 256), BF16),
        ((4, 4, 256, 128), BF16),
        ((2, 2, 4, 64, 128), BF16),
        ((2, 2, 4, 128, 128), BF16),
        ((2, 2, 64, 128), BF16),
        ((2, 2, 128, 128), BF16),
        ((2, 2, 256, 128), BF16),
        ((512, 128), F32),
        ((512, 256), F32),
        ((512, 256), BF16),
        ((512, 256), BF16),
        ((256, 512), BF16),
        ((256, 512), BF16),
        ((4, 128, 256), BF16),
        ((3, 128, 256), BF16),
        ((4, 4, 2, 128, 256), BF16),
        ((4, 4, 512, 256), BF16),
        ((2, 2, 4, 128, 256), BF16),
        ((2, 2, 4, 256, 256), BF16),
        ((2, 2, 128, 256), BF16),
        ((2, 2, 256, 256), BF16),
        ((512, 256), F32),
        ((8, 4, 64, 1024), BF16),
        ((8, 64, 1024), BF16),
        ((8, 64, 1024), BF16),
        ((8, 64, 1024), BF16),
        ((2, 4, 256, 256), BF16),
        ((2, 256, 256), BF16),
        ((2, 256, 256), BF16),
        ((2, 256, 256), BF16),
    ]
    att, gtok, gq, gk, gv = pl.pallas_call(
        kernel,
        name="step",
        out_shape=(
            jax.ShapeDtypeStruct((512, 256), BF16),
            jax.ShapeDtypeStruct((512, 256), BF16),
            jax.ShapeDtypeStruct((64, 8192), BF16),
            jax.ShapeDtypeStruct((256, 256), BF16),
            jax.ShapeDtypeStruct((256, 256), BF16),
        ),
        in_specs=[vmem, vmem, any_space] + [vmem] * 6,
        out_specs=(vmem,) * 5,
        scratch_shapes=[pltpu.VMEM(shape, dtype) for shape, dtype in scratch]
        + [dma((N_SEMS,)), dma((N_SEMS,)), dma],
        compiler_params=pltpu.CompilerParams(
            collective_id=0, has_side_effects=True, vmem_limit_bytes=67043328
        ),
    )(
        tokens, cotangent, w_query.reshape(4, 4, 2, 256, 256), w_key, w_value,
        mask_query.T, mask_key, mask_value, documents,
    )
    att, gtok, gq, gk, gv = hand_out(att, gtok, gq, gk, gv)
    return att, gtok, gq.T, gk, gv


def hand_out_kernel(*refs):
    srcs, dsts, bufs, in_sem, out_sem = refs[:5], refs[5:10], refs[10:15], refs[15], refs[16]
    pieces = []
    for src, dst, buf in zip(srcs, dsts, bufs):
        n = max(1, src.shape[1] // 4096)
        w = src.shape[1] // n
        for i in range(n):
            cols = pl.ds(i * w, w)
            pieces.append((src.at[:, cols], buf.at[:, cols], dst.at[:, cols]))
    fetches = [
        pltpu.make_async_copy(src, buf, in_sem.at[i]) for i, (src, buf, _) in enumerate(pieces)
    ]
    puts = [
        pltpu.make_async_copy(buf, dst, out_sem.at[i]) for i, (_, buf, dst) in enumerate(pieces)
    ]
    for fetch in fetches:
        fetch.start()
    for fetch, put in zip(fetches, puts):
        fetch.wait()
        put.start()
    for put in puts:
        put.wait()


def hand_out(*arrays):
    any_space = pl.BlockSpec(memory_space=pl.ANY)
    return pl.pallas_call(
        hand_out_kernel,
        name="hand_out",
        out_shape=tuple(jax.ShapeDtypeStruct(a.shape, a.dtype) for a in arrays),
        in_specs=[any_space] * 5,
        out_specs=(any_space,) * 5,
        scratch_shapes=[pltpu.VMEM(a.shape, a.dtype) for a in arrays]
        + [pltpu.SemaphoreType.DMA((6,)), pltpu.SemaphoreType.DMA((6,))],
    )(*arrays)


def solution(mesh):
    in_specs = (
        P("seq", "tp"),
        P("seq", "tp"),
        P(None, "tp"),
        P("tp", None),
        P("tp", None),
        P(None, "tp"),
        P("tp", None),
        P("tp", None),
        P("seq", None),
    )
    out_specs = (
        P("seq", "tp"),
        P("seq", "tp"),
        P(None, ("tp", "seq")),
        P("tp", "seq"),
        P("tp", "seq"),
    )
    return jax.shard_map(
        on_device, mesh=mesh, in_specs=in_specs, out_specs=out_specs, check_vma=False
    )
```

```python
import functools

import jax
import jax.numpy as jnp
from jax import lax
from jax.experimental import pallas as pl
from jax.experimental.pallas import tpu as pltpu
from jax.sharding import PartitionSpec as P

MESH = pl.DeviceIdType.MESH
F32 = jnp.float32
BF16 = jnp.bfloat16
HD = 128
BLK = 64
L = 512
N_SEMS = 240


def nt(a, b):
    return lax.dot_general(a, b, (((1,), (1,)), ((), ())), preferred_element_type=F32)


def tn(a, b):
    return lax.dot_general(a, b, (((0,), (0,)), ((), ())), preferred_element_type=F32)


def nn(a, b):
    return jnp.dot(a, b, preferred_element_type=F32)


def add_to(ref, idx, *terms):
    total = ref[idx].astype(F32)
    for term in terms:
        total = total + term.astype(F32)
    ref[idx] = total.astype(BF16)


def drive(gens, times=1):
    for _ in range(times):
        for g in gens:
            next(g, None)


def finish(gens):
    live = list(gens)
    while live:
        for g in list(live):
            if next(g, StopIteration) is StopIteration:
                live.remove(g)


class Links:
    def __init__(self, send_sem, recv_sem):
        self.s = lax.axis_index("seq")
        t = lax.axis_index("tp")
        self.y = lax.div(t, 8)
        self.z = lax.rem(lax.div(t, 2), 4)
        self.c = lax.rem(t, 2)
        self.send_sem, self.recv_sem = send_sem, recv_sem
        self.count = 0
        self.sent = []

    def at(self, dx=0, dy=0, dz=0, flip=False):
        x = lax.rem(self.s + (dx + 4), 4)
        y = lax.rem(self.y + (dy + 4), 4)
        z = lax.rem(self.z + (dz + 4), 4)
        c = 1 - self.c if flip else self.c
        return (x, (y * 4 + z) * 2 + c)

    def wrap(self, base, offset):
        return lax.rem(base + (offset + 8), 4)

    def send(self, src, dst, device):
        k = self.count
        self.count += 1
        copy = pltpu.make_async_remote_copy(
            src_ref=src,
            dst_ref=dst,
            send_sem=self.send_sem.at[k],
            recv_sem=self.recv_sem.at[k],
            device_id=device,
            device_id_type=MESH,
        )
        copy.start()
        self.sent.append(copy)
        return copy

    def drain(self):
        for copy in self.sent:
            copy.wait_send()


def gather_half(lk, buf, half, rows, sib):
    h, q = rows // 2, rows // 4
    base = half * h

    def slot(a, b):
        if half == 0:
            return lk.wrap(lk.y, -a), lk.wrap(lk.z, -b)
        return lk.wrap(lk.y, -b), lk.wrap(lk.z, -a)

    def ref(a, b, r0, n):
        yi, zi = slot(a, b)
        return buf.at[yi, zi, lk.c, pl.ds(base + r0, n), :]

    def near(first, step):
        along_y = first == (half == 0)
        return lk.at(dy=step) if along_y else lk.at(dz=step)

    def snd(a, b, r0, n, dev):
        return lk.send(ref(a, b, r0, n), ref(a, b, r0, n), dev)

    def across(a):
        return snd(a, 0, 0, h, near(False, 1)), snd(a, 0, 0, h, near(False, -1))

    def share(a, b):
        sib.append(snd(a, b, 0, h, lk.at(flip=True)))

    far = {}
    up = snd(0, 0, 0, h, near(True, 1))
    down = snd(0, 0, 0, h, near(True, -1))
    yield
    far[0] = across(0)
    yield
    up.wait_recv()
    up2 = snd(1, 0, 0, q, near(True, 1))
    far[1] = across(1)
    share(1, 0)
    yield
    down.wait_recv()
    down2 = snd(-1, 0, q, q, near(True, -1))
    far[-1] = across(-1)
    share(-1, 0)
    yield
    up2.wait_recv()
    down2.wait_recv()
    far[2] = across(2)
    share(2, 0)
    yield
    last = {}
    for a in (0, 1, -1, 2):
        far[a][0].wait_recv()
        one = snd(a, 1, 0, q, near(False, 1))
        share(a, 1)
        yield
        far[a][1].wait_recv()
        last[a] = one, snd(a, -1, q, q, near(False, -1))
        share(a, -1)
        yield
    for a in (0, 1, -1, 2):
        last[a][0].wait_recv()
        last[a][1].wait_recv()
        share(a, 2)
        yield


def scatter_half(lk, buf, half, rows, t1, t2, t3, t4, result):
    h, q = rows // 2, rows // 4
    base = half * h

    def group(a, r0, n):
        if half == 0:
            return buf.at[:, lk.wrap(lk.z, a), pl.ds(base + r0, n), :]
        return buf.at[lk.wrap(lk.y, a), :, pl.ds(base + r0, n), :]

    def idx(a, i, r0, n):
        if half == 0:
            return (i, lk.wrap(lk.z, a), pl.ds(base + r0, n), slice(None))
        return (lk.wrap(lk.y, a), i, pl.ds(base + r0, n), slice(None))

    def one(b, r0, n):
        if half == 0:
            return (lk.wrap(lk.y, b), lk.z, pl.ds(base + r0, n), slice(None))
        return (lk.y, lk.wrap(lk.z, b), pl.ds(base + r0, n), slice(None))

    def near(first, step):
        along_z = first == (half == 0)
        return lk.at(dz=step) if along_z else lk.at(dy=step)

    e1p = lk.send(group(2, 0, q), t1.at[half, 0], near(True, 1))
    e1m = lk.send(group(2, q, q), t1.at[half, 1], near(True, -1))
    yield
    e1p.wait_recv()
    for i in range(4):
        add_to(buf, idx(1, i, 0, q), t1[half, 0, i])
    e2p = lk.send(group(1, 0, h), t2.at[half, 0], near(True, 1))
    yield
    e1m.wait_recv()
    for i in range(4):
        add_to(buf, idx(-1, i, q, q), t1[half, 1, i])
    e2m = lk.send(group(-1, 0, h), t2.at[half, 1], near(True, -1))
    yield
    e2p.wait_recv()
    e2m.wait_recv()
    for i in range(4):
        add_to(buf, idx(0, i, 0, h), t2[half, 0, i], t2[half, 1, i])
    e3p = lk.send(buf.at[one(2, 0, q)], t3.at[half, 0], near(False, 1))
    e3m = lk.send(buf.at[one(2, q, q)], t3.at[half, 1], near(False, -1))
    yield
    e3p.wait_recv()
    add_to(buf, one(1, 0, q), t3[half, 0])
    e4p = lk.send(buf.at[one(1, 0, h)], t4.at[half, 0], near(False, 1))
    e3m.wait_recv()
    add_to(buf, one(-1, q, q), t3[half, 1])
    e4m = lk.send(buf.at[one(-1, 0, h)], t4.at[half, 1], near(False, -1))
    yield
    e4p.wait_recv()
    e4m.wait_recv()
    total = buf[one(0, 0, h)].astype(F32)
    result(base, h, total + t4[half, 0].astype(F32) + t4[half, 1].astype(F32))


class RingSum:
    def __init__(self, lk, buf, relay, final, other, way):
        self.lk, self.buf, self.way = lk, buf, way
        self.relay_buf, self.final_buf, self.other_buf = relay, final, other
        s = lk.s
        self.raw = lk.send(buf.at[lk.wrap(s, 2)], relay, lk.at(dx=way))
        self.direct = lk.send(buf.at[lk.wrap(s, -way)], other, lk.at(dx=-way))

    def relay(self):
        lk = self.lk
        self.raw.wait_recv()
        mine = lk.wrap(lk.s, self.way)
        add_to(self.buf, (mine,), self.relay_buf[...])
        self.done = lk.send(self.buf.at[mine], self.final_buf, lk.at(dx=self.way))

    def result(self):
        self.done.wait_recv()
        self.direct.wait_recv()
        total = self.buf[self.lk.s].astype(F32)
        return total + self.final_buf[...].astype(F32) + self.other_buf[...].astype(F32)


def kernel(
    tok, cot, wq_hbm, wk, wv, mask_q, mask_k, mask_v, docs,
    att, gtok, gq_out, gk_out, gv_out,
    g, mq, mqs, mkv, mw, mws, mexp, mrow, qf, qb, kvp, kvt1, kvt2, kvt3, kvt4, kvh,
    doc_col, dkf, dq, dqs, dqt, tokt, dkvp, dkvt, dkv, dx, dxt1, dxt2, dxt3, dxt4, dxkv,
    gq, gqr, gqf, gqo, gkv, gkvr, gkvf, gkvo,
    send_sem, recv_sem, local_sem,
):
    lk = Links(send_sem, recv_sem)
    y, z, c, s = lk.y, lk.z, lk.c, lk.s
    scale = HD ** (-0.5)
    zp = lax.rem(z, 2)
    z_mate = z + 1 - 2 * zp
    sibling = lk.at(flip=True)
    mate = (s, (y * 4 + z_mate) * 2 + c)
    cross = (s, (y * 4 + z_mate) * 2 + 1 - c)

    weights = pltpu.make_async_copy(wq_hbm, mq, local_sem)
    weights.start()
    barrier = pltpu.get_barrier_semaphore()
    friends = [sibling, cross, lk.at(dy=1), lk.at(dy=-1), lk.at(dz=1), lk.at(dz=-1), lk.at(dx=1), lk.at(dx=-1)]
    for friend in friends:
        pl.semaphore_signal(barrier, inc=1, device_id=friend, device_id_type=MESH)

    lane = lax.div(lax.broadcasted_iota(jnp.int32, (4, 1024), 1), BLK)
    for kind, (w, m) in enumerate(((wk, mask_k), (wv, mask_v))):
        wide = jnp.zeros((4, 1024), F32)
        for j in range(16):
            wide = jnp.where(lane == j, m[:, j : j + 1].astype(F32), wide)
        for b in range(4):
            rows = slice(b * BLK, (b + 1) * BLK)
            masked = (w[rows, :].astype(F32) * wide[b : b + 1, :]).astype(BF16)
            mw[kind, rows, :] = masked
            for head in range(8):
                mkv[head, rows, kind * HD : (kind + 1) * HD] = masked[:, head * HD : (head + 1) * HD]
    g[y, z, c] = tok[...]
    pl.semaphore_wait(barrier, len(friends))

    sib_tok = lk.send(tok, g.at[y, z, c], sibling)
    sib_w = lk.send(mw.at[1 - c], mws, sibling)
    shared = []
    ga = gather_half(lk, g, 0, L, shared)
    gb = gather_half(lk, g, 1, L, shared)
    drive((ga, gb), 2)

    lane = lax.div(lax.broadcasted_iota(jnp.int32, (128, 256), 1), BLK)
    row = lax.broadcasted_iota(jnp.int32, (128, 128), 0)
    cols = jnp.zeros((128, 128), F32)
    own = jnp.zeros((8, 128), F32)
    for j in range(4):
        line = mask_q[j : j + 1, :].astype(F32)
        cols = jnp.where(row == j, line, cols)
        own = jnp.where(s == j, line, own)
    cols = cols.T
    wide = jnp.zeros((128, 256), F32)
    for j in range(4):
        wide = jnp.where(lane == j, cols[:, j : j + 1], wide)
    mexp[...] = wide
    own = own.astype(BF16)
    ahead = lax.broadcasted_iota(jnp.int32, (128, 1024), 0) - lax.div(
        lax.broadcasted_iota(jnp.int32, (128, 1024), 1), BLK
    )
    for j in range(8):
        mrow[:, j * 1024 : (j + 1) * 1024] = nn(own, jnp.where(ahead == 16 * j, 1.0, 0.0).astype(BF16))
    weights.wait()

    def mask_chunk(t, carry):
        yi, zi, ci = lax.div(t, 8), lax.rem(lax.div(t, 2), 4), lax.rem(t, 2)
        for b in range(4):
            rows = slice(b * BLK, (b + 1) * BLK)
            line = mexp[pl.ds(4 * t + b, 1), :]
            mq[yi, zi, ci, rows, :] = (mq[yi, zi, ci, rows, :].astype(F32) * line).astype(BF16)
        return carry

    lax.fori_loop(0, 32, mask_chunk, 0)
    sib_mq = lk.send(mq.at[:, :, 1 - c], mqs, sibling)

    sib_tok.wait_recv()
    sib_w.wait_recv()

    def kv_pair(i, carry):
        cols = pl.ds(pl.multiple_of(i * 256, 256), 256)
        part = nn(tok[...], mw[c, :, cols]) + nn(g[y, z, 1 - c], mws[:, cols])
        part = part.astype(BF16)
        for hh in range(2):
            for th in range(2):
                kvp[i, 2 * hh + th] = part[th * 256 : (th + 1) * 256, hh * HD : (hh + 1) * HD]
        return carry

    lax.fori_loop(0, 4, kv_pair, 0)

    def store_kv(base, n, value):
        kvh[c, zp, base : base + n, :] = value.astype(BF16)

    ka = scatter_half(lk, kvp, 0, 256, kvt1, kvt2, kvt3, kvt4, store_kv)
    kb = scatter_half(lk, kvp, 1, 256, kvt1, kvt2, kvt3, kvt4, store_kv)
    drive((ka, kb))
    drive((ga, gb), 3)
    drive((ka, kb), 2)

    qf[...] = jnp.zeros_like(qf)

    def project(yi, zi, ci):
        qf[...] += nn(g[yi, zi, ci], mq[yi, zi, ci])

    project(y, z, c)
    project(y, z, 1 - c)
    drive((ga, gb), 2)
    drive((ka, kb))
    drive((ga, gb), 2)
    finish((ka, kb))
    hand = [lk.send(kvh.at[c, zp], kvh.at[c, zp], dev) for dev in (sibling, mate, cross)]
    tokt[...] = tok[...].astype(F32).T.astype(BF16)
    finish((ga, gb))

    def project_own(i, carry):
        yi, zi = lax.div(i, 4), lax.rem(i, 4)
        project(lk_wrap(y, yi), lk_wrap(z, zi), c)
        return carry

    def lk_wrap(base, offset):
        return lax.rem(base + offset, 4)

    lax.fori_loop(1, 16, project_own, 0)
    for copy in shared:
        copy.wait_recv()

    def project_sib(i, carry):
        yi, zi = lax.div(i, 4), lax.rem(i, 4)
        project(lk_wrap(y, yi), lk_wrap(z, zi), 1 - c)
        return carry

    lax.fori_loop(1, 16, project_sib, 0)
    qb[...] = qf[...].astype(BF16)
    for copy in hand:
        copy.wait_recv()

    doc_row = docs[...]
    doc_col[...] = jnp.broadcast_to(doc_row.astype(F32), (128, L)).T
    for h in range(2):
        hs = slice(h * HD, (h + 1) * HD)
        for rb in (1, 0):
            rows, nk = slice(rb * 256, rb * 256 + 256), rb * 256 + 256
            kk = kvh[0].reshape(L, HD)[:nk]
            vv = kvh[1].reshape(L, HD)[:nk]
            qh, gh = qb[rows, hs], cot[rows, hs]
            ri = lax.broadcasted_iota(jnp.int32, (256, nk), 0) + rb * 256
            ci = lax.broadcasted_iota(jnp.int32, (256, nk), 1)
            same = doc_col[rows, 0:1] == doc_row[:, :nk].astype(F32)
            allowed = jnp.logical_and(same, ci <= ri)
            w = jnp.where(allowed, jnp.exp(nt(qh, kk) * scale), 0.0)
            probs = w * (1.0 / jnp.sum(w, axis=1, keepdims=True))
            pb = probs.astype(BF16)
            att[rows, hs] = nn(pb, vv).astype(BF16)
            da = nt(gh, vv)
            ds = probs * (da - jnp.sum(da * probs, axis=1, keepdims=True)) * scale
            ds = ds.astype(BF16)
            dq[rows, hs] = nn(ds, kk).astype(BF16)
            dk_part, dv_part = tn(ds, qh), tn(pb, gh)
            if h == 0 and rb == 1:
                dkf[:nk, :HD] = dk_part
                dkf[:nk, HD:] = dv_part
            else:
                dkf[:nk, :HD] += dk_part
                dkf[:nk, HD:] += dv_part
    dkvp[...] = dkf[...].astype(BF16).reshape(4, 128, 256)

    sib_dq = lk.send(dq, dqs, sibling)
    quarter = 2 * zp + c
    swaps = []
    for i, (dev, qi) in enumerate(
        ((sibling, 2 * zp + 1 - c), (mate, 2 * (1 - zp) + c), (cross, 2 * (1 - zp) + 1 - c))
    ):
        swaps.append(lk.send(dkvp.at[qi], dkvt.at[i], dev))
    dqt[...] = dq[...].astype(F32).T.astype(BF16)

    rings = []

    def grad_query_group(j):
        for i in range(4):
            t = 4 * j + i
            part = nn(dqt[...], g[t // 8, (t // 2) % 4, t % 2]).astype(BF16)
            gq[j, :, :, i * 256 : (i + 1) * 256] = part.reshape(4, BLK, 256)
        rings.append(RingSum(lk, gq.at[j], gqr.at[j], gqf.at[j], gqo.at[j], 1 - 2 * (j % 2)))

    grad_query_group(0)
    grad_query_group(1)
    for copy in swaps:
        copy.wait_recv()
    total = dkvp[quarter].astype(F32)
    for i in range(3):
        total = total + dkvt[i].astype(F32)
    dkv[y, z, c] = total.astype(BF16)
    shared2 = [lk.send(dkv.at[y, z, c], dkv.at[y, z, c], sibling)]
    da_ = gather_half(lk, dkv, 0, 128, shared2)
    db_ = gather_half(lk, dkv, 1, 128, shared2)
    drive((da_, db_), 2)
    grad_query_group(2)
    grad_query_group(3)
    drive((da_, db_), 2)

    sib_mq.wait_recv()
    sib_dq.wait_recv()

    def dx_slot(yi, zi):
        part = nt(dq[...], mq[yi, zi, c]) + nt(dqs[...], mqs[yi, zi])
        dx[yi, zi] = part.astype(BF16)

    def dx_far_z(i, carry):
        dx_slot(i, lk_wrap(z, 2))
        return carry

    def dx_far_y(i, carry):
        dx_slot(lk_wrap(y, 2), lk_wrap(z, 2 + i))
        return carry

    def dx_near(i, carry):
        dx_slot(lk_wrap(y, 3 + lax.div(i, 3)), lk_wrap(z, 3 + lax.rem(i, 3)))
        return carry

    def store_dx(base, n, value):
        rows = slice(base, base + n)
        gtok[rows, :] = (value + dxkv[rows, :]).astype(BF16)

    xa = scatter_half(lk, dx, 0, L, dxt1, dxt2, dxt3, dxt4, store_dx)
    xb = scatter_half(lk, dx, 1, L, dxt1, dxt2, dxt3, dxt4, store_dx)
    lax.fori_loop(0, 4, dx_far_z, 0)
    drive((xa,))
    lax.fori_loop(1, 4, dx_far_y, 0)
    drive((xb,))
    grad_query_group(4)
    grad_query_group(5)
    drive((da_, db_), 1)
    grad_query_group(6)
    grad_query_group(7)
    lax.fori_loop(0, 9, dx_near, 0)
    drive((da_, db_), 4)
    drive((xa, xb))
    drive((da_, db_), 4)
    drive((xa, xb))
    rings[0].relay()
    rings[1].relay()
    finish((da_, db_))
    for copy in shared2:
        copy.wait_recv()

    for p in range(4):
        for hh in range(2):
            zi = 2 * hh
            pair = jnp.concatenate(
                [dkv[p, zi, 0], dkv[p, zi, 1], dkv[p, zi + 1, 0], dkv[p, zi + 1, 1]], axis=0
            )
            part = nn(tokt[...], pair).astype(BF16)
            gkv[0, p, :, hh * HD : (hh + 1) * HD] = part[:, :HD]
            gkv[1, p, :, hh * HD : (hh + 1) * HD] = part[:, HD:]
            more = nt(pair, mkv[2 * p + hh])
            if p == 0 and hh == 0:
                dxkv[...] = more
            else:
                dxkv[...] += more
    kv_rings = [
        RingSum(lk, gkv.at[i], gkvr.at[i], gkvf.at[i], gkvo.at[i], 1 - 2 * i) for i in range(2)
    ]
    for ring in rings[2:4]:
        ring.relay()
    drive((xa, xb))
    for ring in rings[4:6]:
        ring.relay()
    drive((xa, xb))
    for ring in rings[6:8]:
        ring.relay()
    finish((xa, xb))
    for ring in kv_rings:
        ring.relay()
    for j, ring in enumerate(rings):
        cols = slice(j * 1024, (j + 1) * 1024)
        gq_out[:, cols] = (ring.result() * mrow[0:1, cols]).astype(BF16)
    lane = lax.div(lax.broadcasted_iota(jnp.int32, (4, 256), 1), BLK)
    col = lax.broadcasted_iota(jnp.int32, (4, 16), 1)
    for ring, m, out in ((kv_rings[0], mask_k, gk_out), (kv_rings[1], mask_v, gv_out)):
        wide = jnp.zeros((4, 256), F32)
        for j in range(4):
            pick = jnp.sum(jnp.where(col == 4 * s + j, m[...].astype(F32), 0.0), axis=1, keepdims=True)
            wide = jnp.where(lane == j, pick, wide)
        total = ring.result()
        for b in range(4):
            rows = slice(b * BLK, (b + 1) * BLK)
            out[rows, :] = (total[rows, :] * wide[b : b + 1, :]).astype(BF16)
    lk.drain()


def on_device(tokens, cotangent, w_query, w_key, w_value, mask_query, mask_key, mask_value, documents):
    vmem = pl.BlockSpec(memory_space=pltpu.VMEM)
    any_space = pl.BlockSpec(memory_space=pl.ANY)
    dma = pltpu.SemaphoreType.DMA
    scratch = [
        ((4, 4, 2, 512, 256), BF16),
        ((4, 4, 2, 256, 256), BF16),
        ((4, 4, 256, 256), BF16),
        ((8, 256, 256), BF16),
        ((2, 256, 1024), BF16),
        ((256, 1024), BF16),
        ((128, 256), F32),
        ((8, 8192), F32),
        ((512, 256), F32),
        ((512, 256), BF16),
        ((4, 4, 256, 128), BF16),
        ((2, 2, 4, 64, 128), BF16),
        ((2, 2, 4, 128, 128), BF16),
        ((2, 2, 64, 128), BF16),
        ((2, 2, 128, 128), BF16),
        ((2, 2, 256, 128), BF16),
        ((512, 128), F32),
        ((512, 256), F32),
        ((512, 256), BF16),
        ((512, 256), BF16),
        ((256, 512), BF16),
        ((256, 512), BF16),
        ((4, 128, 256), BF16),
        ((3, 128, 256), BF16),
        ((4, 4, 2, 128, 256), BF16),
        ((4, 4, 512, 256), BF16),
        ((2, 2, 4, 128, 256), BF16),
        ((2, 2, 4, 256, 256), BF16),
        ((2, 2, 128, 256), BF16),
        ((2, 2, 256, 256), BF16),
        ((512, 256), F32),
        ((8, 4, 64, 1024), BF16),
        ((8, 64, 1024), BF16),
        ((8, 64, 1024), BF16),
        ((8, 64, 1024), BF16),
        ((2, 4, 256, 256), BF16),
        ((2, 256, 256), BF16),
        ((2, 256, 256), BF16),
        ((2, 256, 256), BF16),
    ]
    att, gtok, gq, gk, gv = pl.pallas_call(
        kernel,
        name="step",
        out_shape=(
            jax.ShapeDtypeStruct((512, 256), BF16),
            jax.ShapeDtypeStruct((512, 256), BF16),
            jax.ShapeDtypeStruct((64, 8192), BF16),
            jax.ShapeDtypeStruct((256, 256), BF16),
            jax.ShapeDtypeStruct((256, 256), BF16),
        ),
        in_specs=[vmem, vmem, any_space] + [vmem] * 6,
        out_specs=(vmem,) * 5,
        scratch_shapes=[pltpu.VMEM(shape, dtype) for shape, dtype in scratch]
        + [dma((N_SEMS,)), dma((N_SEMS,)), dma],
        compiler_params=pltpu.CompilerParams(
            collective_id=0, has_side_effects=True, vmem_limit_bytes=67043328
        ),
    )(
        tokens, cotangent, w_query.reshape(4, 4, 2, 256, 256), w_key, w_value,
        mask_query.T, mask_key, mask_value, documents,
    )
    att, gtok, gq, gk, gv = hand_out(att, gtok, gq, gk, gv)
    return att, gtok, gq.T, gk, gv


def hand_out_kernel(*refs):
    srcs, dsts, bufs, in_sem, out_sem = refs[:5], refs[5:10], refs[10:15], refs[15], refs[16]
    pieces = []
    for src, dst, buf in zip(srcs, dsts, bufs):
        n = max(1, src.shape[1] // 4096)
        w = src.shape[1] // n
        for i in range(n):
            cols = pl.ds(i * w, w)
            pieces.append((src.at[:, cols], buf.at[:, cols], dst.at[:, cols]))
    fetches = [
        pltpu.make_async_copy(src, buf, in_sem.at[i]) for i, (src, buf, _) in enumerate(pieces)
    ]
    puts = [
        pltpu.make_async_copy(buf, dst, out_sem.at[i]) for i, (_, buf, dst) in enumerate(pieces)
    ]
    for fetch in fetches:
        fetch.start()
    for fetch, put in zip(fetches, puts):
        fetch.wait()
        put.start()
    for put in puts:
        put.wait()


def hand_out(*arrays):
    any_space = pl.BlockSpec(memory_space=pl.ANY)
    return pl.pallas_call(
        hand_out_kernel,
        name="hand_out",
        out_shape=tuple(jax.ShapeDtypeStruct(a.shape, a.dtype) for a in arrays),
        in_specs=[any_space] * 5,
        out_specs=(any_space,) * 5,
        scratch_shapes=[pltpu.VMEM(a.shape, a.dtype) for a in arrays]
        + [pltpu.SemaphoreType.DMA((6,)), pltpu.SemaphoreType.DMA((6,))],
    )(*arrays)


def solution(mesh):
    in_specs = (
        P("seq", "tp"),
        P("seq", "tp"),
        P(None, "tp"),
        P("tp", None),
        P("tp", None),
        P(None, "tp"),
        P("tp", None),
        P("tp", None),
        P("seq", None),
    )
    out_specs = (
        P("seq", "tp"),
        P("seq", "tp"),
        P(None, ("tp", "seq")),
        P("tp", "seq"),
        P("tp", "seq"),
    )
    return jax.shard_map(
        on_device, mesh=mesh, in_specs=in_specs, out_specs=out_specs, check_vma=False
    )
```
